32 devices in a mesh: grp: 4 (over y, x), dev: 8 (over z, core).
Axes of the slice: x: 2, y: 2, z: 4, core: 2. Of those that a mesh axis runs over, the one named last changes fastest.
Arguments:
- reach: bfloat16 [128, 64, 1326], P(('grp', 'dev')), may hold values from 0.00029945374 to 0.0029907227
- stake: float32 [128], replicated, may hold values from 1 to 10
- hand_rank: int32 [64, 1326], P(('grp', 'dev')), may hold values from 0 to 7461
- hand_live: int32 [64, 1326], P(('grp', 'dev')), may hold values 0 or 1
- board_seqs: int32 [64], P(('grp', 'dev')), may hold values from 1 to 128, 4096 in all
- board_turn: int32 [64, 1], replicated, may hold values from 0 to 15
- seq_parent: int32 [128], replicated, may hold values from 0 to 31, never falling along the last dimension, each value on 1 to 8 neighbouring positions
- set_parent: int32 [32], replicated, may hold values from 0 to 7, never falling along the last dimension, each value on 1 to 8 neighbouring positions
Outputs:
- river_values: float32 [32, 64, 1326], P(None, ('grp', 'dev'))
- turn_values: float32 [8, 16, 1326], replicated
The draws below stay inside these ranges and needn't reach their ends.
Inputs may be any that keep to these rules, and one draw needn't show every extreme that they name: `seq_parent`: Non-decreasing; every value occurs, at most 8 times, exactly 8 times for some value. `set_parent`: Non-decreasing; every value occurs, at most 8 times, exactly 8 times for some value. `board_seqs`: some board has all 128 sequences live. `board_turn`: every turn board has at least one river board.
All inputs are finite; a program needn't handle non-finite values. No bound on the sum of `hand_live` or of `board_seqs` on one device may be relied on, other than what follows from the above.
Results may differ from the reference program's by a relative error of at most 0.0003.
Values may be sent and summed in bfloat16 or wider, within the bound.
A program may use at most 64 MiB of HBM per device.

```python
import math
import jax
import jax.numpy as jnp
import numpy as np
from jax import lax

H = 1326
TURNS = 16
SET_KIDS = 8
SEQ = 128
BOARDS = 64
RIV_SETS = 32
KIDS = 8
TURN_SETS = 8


def touch_ends(values, stream_key, smallest, high):
    longest = values.shape.index(max(values.shape))
    spots = []
    for shift in (0, 1):
        where = [jax.random.randint(jax.random.fold_in(stream_key, axis), (), 0, length) for axis, length in enumerate(values.shape)]
        where[longest] = (where[longest] + shift) % values.shape[longest]
        spots.append(tuple(where))
    return values.at[spots[0]].set(smallest).at[spots[1]].set(high)


def block_scale(own_key, shape, shards, smallest, largest):
    gain, own = 1.0, jax.random.fold_in(own_key, 6)
    for dim, shards_of in shards:
        draws = jnp.exp(jax.random.uniform(jax.random.fold_in(own, dim), (shards_of,), jnp.float32, smallest / len(shards), largest / len(shards)))
        gain = gain * jnp.repeat(draws, shape[dim] // shards_of).reshape([-1 if axis == dim else 1 for axis in range(len(shape))])
    return gain


def distinct(rng, rows, count, top, lift):
    order = jax.random.permutation(jax.random.fold_in(rng, 1), count)
    pull = order
    for power in range(3):
        pull = pull * pull // count
    pull = pull * lift // count
    chance = jax.random.randint(jax.random.fold_in(rng, 2), (rows, count), 0, 4096) + pull
    sure = jax.random.permutation(jax.random.fold_in(rng, 3), rows)[jnp.arange(count) % rows]
    chance = jnp.where(jnp.arange(rows)[:, None] == sure[None, :], 1 << 14, chance)
    priority = chance * count + jnp.arange(count)
    return lax.top_k(priority.astype(jnp.int32), top)[1].astype(jnp.int32)


def profile(number_of, total, most, slope):
    weights = [(1 << 20) // math.isqrt(rank ** slope) + 1 for rank in range(2, number_of + 1)]
    spare, given = total - most - (number_of - 1), [1] * (number_of - 1)
    while spare > 0:
        movable = [i for i in range(number_of - 1) if given[i] < most]
        mass, left = sum([weights[i] for i in movable]), spare
        for i in movable:
            addition = min(most - given[i], max(1, left * weights[i] // mass), spare)
            given[i] = given[i] + addition
            spare = spare - addition
    return np.array([most] + given)


def uneven(own_key, amount, total, most, slope):
    if amount == 2:
        one = jax.random.randint(own_key, (), max(1, total - most), min(most, total - 1) + 1)
        return jnp.stack([one, total - one])
    lengths = jnp.asarray(profile(amount, total, most, slope), jnp.int32)
    pairs = (amount - 1) // 2
    donor, taker = lengths[1:1 + 2 * pairs:2], lengths[2:2 + 2 * pairs:2]
    room = jnp.minimum(donor - 1, most - taker)
    passed = jax.random.randint(jax.random.fold_in(own_key, 1), (pairs,), 0, 1 << 20) % (room + 1)
    lengths = lengths.at[1:1 + 2 * pairs:2].set(donor - passed).at[2:2 + 2 * pairs:2].set(taker + passed)
    return lengths[jax.random.permutation(jax.random.fold_in(own_key, 2), amount)]


def setup_inputs(seed: int = 0) -> dict:
    key_list = jax.random.split(jax.random.key(seed), 9)
    return {
        "reach": jnp.clip(jnp.exp(math.log(0.0029907227) - 2.3013104 * jax.random.uniform(key_list[0], (SEQ, BOARDS, H), jnp.float32) ** block_scale(key_list[0], (SEQ, BOARDS, H), ((0, 32),), -0.2, 0.2)), 0.00029945374, 0.0029907227).astype(jnp.bfloat16),
        "stake": jnp.clip(jnp.exp(jax.random.uniform(key_list[1], (SEQ,), jnp.float32, math.log(1.0), math.log(10.0))), 1.0, 10.0),
        "hand_rank": touch_ends(jax.random.randint(key_list[2], (BOARDS, H), 0, 7462), jax.random.fold_in(key_list[2], 1), 0, 7461).astype(jnp.int32),
        "hand_live": touch_ends((jax.random.randint(key_list[3], (BOARDS, H), 0, 5) < 4).astype(jnp.int32), jax.random.fold_in(key_list[3], 1), 0, 1),
        "board_seqs": uneven(key_list[4], BOARDS, BOARDS * SEQ // 2, SEQ, 2).astype(jnp.int32),
        "board_turn": distinct(key_list[5], BOARDS, TURNS, 1, 0),
        "seq_parent": jnp.searchsorted(jnp.cumsum(uneven(key_list[6], RIV_SETS, SEQ, KIDS, 1)), jnp.arange(SEQ), side="right").astype(jnp.int32),
        "set_parent": jnp.searchsorted(jnp.cumsum(uneven(key_list[7], TURN_SETS, RIV_SETS, SET_KIDS, 1)), jnp.arange(RIV_SETS), side="right").astype(jnp.int32),
    }


def hand_cards(count):
    card_pairs = [(lower_card, upper_card) for lower_card in range(52) for upper_card in range(lower_card + 1, 52)]
    table = np.array(card_pairs[:count], dtype=np.int32)
    return jnp.asarray(table[:, 0]), jnp.asarray(table[:, 1])


def apart_table(count):
    first_card, second_card = hand_cards(count)
    return ((first_card[:, None] != first_card[None, :]) & (first_card[:, None] != second_card[None, :])
            & (second_card[:, None] != first_card[None, :]) & (second_card[:, None] != second_card[None, :]))


def payoff_matrix(ranks, live, apart):
    both_live = (live[:, None] * live[None, :]) > 0
    signs = jnp.sign(ranks[:, None] - ranks[None, :]).astype(jnp.float32)
    return jnp.where(apart & both_live, signs, jnp.float32(0.0))


def children(parent, count_sets, most):
    set_iota = jnp.arange(count_sets, dtype=jnp.int32)
    counts = jnp.sum((parent[None, :] == set_iota[:, None]).astype(jnp.int32), axis=1)
    starts = jnp.cumsum(counts) - counts
    kid_iota = jnp.arange(most, dtype=jnp.int32)
    index = jnp.minimum(starts[:, None] + kid_iota[None, :], parent.shape[0] - 1).astype(jnp.int32)
    valid = kid_iota[None, :] < counts[:, None]
    return index, valid


def segment_best(values, index, valid):
    picked = values[index]
    shape = valid.shape + (1,) * (values.ndim - 1)
    return jnp.max(jnp.where(valid.reshape(shape), picked, -jnp.inf), axis=1)


def reference(reach, stake, hand_rank, hand_live, board_seqs, board_turn, seq_parent, set_parent):
    apart = apart_table(H)
    kid_index, kid_valid = children(seq_parent, RIV_SETS, KIDS)
    seq_iota = jnp.arange(SEQ, dtype=jnp.int32)

    def per_board(board):
        live_rows = (seq_iota < board_seqs[board]).astype(jnp.float32)
        rows = reach[:, board, :].astype(jnp.float32) * live_rows[:, None]
        matrix = payoff_matrix(hand_rank[board], hand_live[board], apart)
        leaf = jnp.dot(rows, matrix.T, precision=lax.Precision.HIGHEST) * stake[:, None]
        return segment_best(leaf, kid_index, kid_valid)

    river = lax.map(per_board, jnp.arange(BOARDS, dtype=jnp.int32))
    river = jnp.transpose(river, (1, 0, 2))
    onehot = (board_turn[:, 0][None, :] == jnp.arange(TURNS, dtype=jnp.int32)[:, None]).astype(jnp.float32)
    chance = jnp.einsum("tb,pbh->pth", onehot, river, precision=lax.Precision.HIGHEST)
    set_index, set_valid = children(set_parent, TURN_SETS, SET_KIDS)
    best = segment_best(chance, set_index, set_valid)
    return river, best
```

```python
import functools

import jax
import jax.numpy as jnp
import numpy as np
from jax import lax
from jax.experimental import pallas as pl
from jax.experimental.pallas import tpu as pltpu
from jax.sharding import PartitionSpec as P

TURNS = 16
KIDS = 8
LANE = 128
MESH = pl.DeviceIdType.MESH


def card_bits(count, padded):
    pairs = [(a, b) for a in range(52) for b in range(a + 1, 52)][:count]
    words = np.zeros((2, padded), np.int32)
    for hand, pair in enumerate(pairs):
        for card in pair:
            words[card // 26, hand] |= 1 << (card % 26)
    return words


def children(parent, count_sets, most):
    set_iota = jnp.arange(count_sets, dtype=jnp.int32)
    starts = jnp.sum((parent[None, :] < set_iota[:, None]).astype(jnp.int32), axis=1)
    ends = jnp.sum((parent[None, :] <= set_iota[:, None]).astype(jnp.int32), axis=1)
    kid_iota = jnp.arange(most, dtype=jnp.int32)
    return jnp.minimum(starts[:, None] + kid_iota[None, :], ends[:, None] - 1)


def kernel(G, D, hands, kids_ref, turn_ref, parent_col, reach_ref, rank_ref, live_ref, bits_ref, scale_ref,
           river_out, turn_out,
           moved, rows_f, rows_i, cols_f, cols_i, pay, leaf, river, gathered, chance, best,
           send_a, recv_a, send_c, recv_c, send_e, recv_e, own_sem):
    n = G * D
    tiles = -(-hands // LANE)
    width = tiles * LANE
    sets = river_out.shape[0]
    turn_sets = turn_out.shape[0]
    g, d = lax.axis_index("grp"), lax.axis_index("dev")
    core = lax.rem(d, 2)
    me = g * D + d

    def where_is(flat):
        return (flat // D, lax.rem(flat, D))

    barrier = pltpu.get_barrier_semaphore()

    @pl.loop(1, n)
    def _(k):
        pl.semaphore_signal(barrier, inc=1, device_id=where_is(lax.rem(me + k, n)), device_id_type=MESH)

    pl.semaphore_wait(barrier, n - 1)

    def send_reach(k):
        to = lax.rem(me + k, n)
        return pltpu.make_async_remote_copy(
            src_ref=reach_ref.at[to], dst_ref=moved.at[me], send_sem=send_a.at[k], recv_sem=recv_a.at[me],
            device_id=where_is(to), device_id_type=MESH)

    def got_reach(k):
        frm = lax.rem(me + k, n)
        return pltpu.make_async_remote_copy(
            src_ref=reach_ref.at[frm], dst_ref=moved.at[frm], send_sem=send_a.at[k], recv_sem=recv_a.at[frm],
            device_id=where_is(frm), device_id_type=MESH)

    own = pltpu.make_async_copy(reach_ref.at[me], moved.at[me], own_sem.at[0])
    own.start()

    @pl.loop(1, n)
    def _(k):
        send_reach(k).start()

    rows_f[...] = jnp.zeros_like(rows_f)
    rows_i[...] = jnp.zeros_like(rows_i)
    rows_f[0:2, 0:hands] = rank_ref[...].astype(jnp.float32)
    rows_i[0:2, 0:hands] = live_ref[...]
    dead = 1 - rows_i[0:2, :]
    low, high = bits_ref[0:1, :], bits_ref[1:2, :]
    ours = low + (1 << 26) + dead * (1 << 27)
    theirs = low + (1 << 27) + dead * (1 << 26)
    rows_i[0:2, :] = ours
    rows_i[2:3, :] = high
    rows_i[3:5, :] = theirs
    for tile in range(tiles):
        cut = slice(tile * LANE, (tile + 1) * LANE)
        cols_f[cut, :] = jnp.transpose(rows_f[:, cut])
        cols_i[cut, :] = jnp.transpose(rows_i[:, cut])

    @pl.loop(0, width // 16)
    def _(step):
        at = pl.ds(pl.multiple_of(step * 16, 16), 16)
        ranks, words = cols_f[at, :], cols_i[at, :]
        for board in range(2):
            shared = (rows_i[board:board + 1, :] & words[:, 3 + board:4 + board]) | (rows_i[2:3, :] & words[:, 2:3])
            sign = jnp.clip(rows_f[board:board + 1, :] - ranks[:, board:board + 1], -1.0, 1.0)
            pay[board, at, :] = jnp.where(shared == 0, sign, 0.0).astype(jnp.bfloat16)

    own.wait()

    @pl.loop(1, n)
    def _(k):
        got_reach(k).wait_recv()

    chunk = 32
    first = lax.broadcasted_iota(jnp.int32, (chunk * 8, 1), 0) % 8 < 4

    @pl.loop(0, n // chunk)
    def _(part):
        src = pl.ds(part * chunk, chunk)
        rows = moved[src].astype(jnp.float32).reshape(chunk * 8, width).astype(jnp.bfloat16)
        at = pl.ds(pl.multiple_of(part * chunk * 8, chunk * 8), chunk * 8)
        scale = scale_ref[at, :]
        for nt in range(leaf.shape[1] // 256):
            cut = slice(nt * 256, (nt + 1) * 256)
            one = jnp.dot(rows, pay[0, :, cut], preferred_element_type=jnp.float32)
            two = jnp.dot(rows, pay[1, :, cut], preferred_element_type=jnp.float32)
            leaf[at, cut] = jnp.where(first, one, two) * scale

    @pl.loop(0, sets)
    def _(p):
        for board in range(2):
            row = leaf[pl.ds(kids_ref[p * KIDS] + 4 * board, 1), 0:width]
            for kid in range(1, KIDS):
                row = jnp.maximum(row, leaf[pl.ds(kids_ref[p * KIDS + kid] + 4 * board, 1), 0:width])
            river[board, pl.ds(p, 1), :] = row
            river_out[p, board:board + 1, :] = row[:, 0:hands]

    zs = (1, 2, 0) + tuple(range(3, D // 2))
    owner_g = [j % G for j in range(tiles)]
    owner_d = [(2 * zs[(j // G) % len(zs)] + (j % G + j // G) % 2) % D for j in range(tiles)]

    def send_river(j):
        return pltpu.make_async_remote_copy(
            src_ref=river.at[:, :, pl.ds(j * LANE, LANE)], dst_ref=gathered.at[pl.ds(2 * me, 2)],
            send_sem=send_c.at[j], recv_sem=recv_c.at[me], device_id=(owner_g[j], owner_d[j]), device_id_type=MESH)

    def is_owner(j):
        return (g == owner_g[j]) & (d == owner_d[j])

    def own_river(j):
        return pltpu.make_async_copy(
            river.at[:, :, pl.ds(j * LANE, LANE)], gathered.at[pl.ds(2 * me, 2)], own_sem.at[1])

    for j in range(tiles):
        @pl.when(is_owner(j))
        def _():
            own_river(j).start()

        @pl.when(jnp.logical_not(is_owner(j)))
        def _():
            send_river(j).start()

    def send_turn(j, slot, to):
        piece = best.at[:, :, pl.ds(j * LANE, LANE)]
        return pltpu.make_async_remote_copy(
            src_ref=piece, dst_ref=piece, send_sem=send_e.at[j, slot], recv_sem=recv_e.at[j],
            device_id=to, device_id_type=MESH)

    def got_turn(j):
        return send_turn(j, 0, (g, d))

    lines = D // 2
    any_owner = functools.reduce(jnp.logical_or, [is_owner(j) for j in range(tiles)])

    @pl.when(any_owner)
    def _():
        pltpu.make_async_copy(river.at[:, :, pl.ds(0, LANE)], gathered.at[pl.ds(2 * me, 2)], own_sem.at[1]).wait()

        @pl.loop(1, n)
        def _(k):
            frm = lax.rem(me + k, n)
            pltpu.make_async_remote_copy(
                src_ref=river.at[:, :, pl.ds(0, LANE)], dst_ref=gathered.at[pl.ds(2 * frm, 2)],
                send_sem=send_c.at[0], recv_sem=recv_c.at[frm], device_id=where_is(frm),
                device_id_type=MESH).wait_recv()

        group = 4
        psub = 32
        for turn0 in range(0, TURNS, group):
            for p0 in range(0, sets, psub):
                def add(b, accs):
                    block = gathered[b, p0:p0 + psub, :]
                    return tuple(
                        acc + jnp.where(turn_ref[b] == turn0 + i, 1.0, 0.0) * block for i, acc in enumerate(accs))
                accs = lax.fori_loop(
                    0, 2 * n, add, tuple(jnp.zeros((psub, LANE), jnp.float32) for _ in range(group)), unroll=8)
                for i in range(group):
                    chance[turn0 + i, p0:p0 + psub, :] = accs[i]

        parents = parent_col[...]

        @pl.loop(0, turn_sets)
        def _(q):
            chosen = parents == q
            rows = [jnp.max(jnp.where(chosen, chance[t], -jnp.inf), axis=0, keepdims=True) for t in range(TURNS)]
            value = jnp.concatenate(rows, axis=0)
            for j in range(tiles):
                @pl.when(is_owner(j))
                def _():
                    best[q, :, pl.ds(j * LANE, LANE)] = value

    def peers(j):
        return [(k, (g, 2 * lax.rem(d // 2 + k, lines) + core)) for k in range(1, lines)]

    def across(j):
        return [(lines - 1 + k, (lax.rem(g + k, G), d)) for k in range(1, G)]

    def pair(j):
        return [(lines - 1 + G, (g, d + 1 - 2 * core))]

    in_line = [(g == owner_g[j]) & (core == owner_d[j] % 2) for j in range(tiles)]
    has_core = [core == owner_d[j] % 2 for j in range(tiles)]
    for j in range(tiles):
        @pl.when(is_owner(j))
        def _():
            for slot, to in peers(j) + across(j) + pair(j):
                send_turn(j, slot, to).start()
    for j in range(tiles):
        @pl.when(in_line[j] & jnp.logical_not(is_owner(j)))
        def _():
            got_turn(j).wait_recv()
            for slot, to in across(j) + pair(j):
                send_turn(j, slot, to).start()
    for j in range(tiles):
        @pl.when(has_core[j] & jnp.logical_not(in_line[j]))
        def _():
            got_turn(j).wait_recv()
            for slot, to in pair(j):
                send_turn(j, slot, to).start()
    for j in range(tiles):
        @pl.when(jnp.logical_not(has_core[j]))
        def _():
            got_turn(j).wait_recv()

    turn_out[...] = best[:, :, 0:hands]

    for j in range(tiles):
        @pl.when(is_owner(j))
        def _():
            for slot, to in peers(j):
                send_turn(j, slot, to).wait_send()

        @pl.when(in_line[j])
        def _():
            for slot, to in across(j):
                send_turn(j, slot, to).wait_send()

        @pl.when(has_core[j])
        def _():
            for slot, to in pair(j):
                send_turn(j, slot, to).wait_send()

        @pl.when(jnp.logical_not(is_owner(j)))
        def _():
            send_river(j).wait_send()

    @pl.loop(1, n)
    def _(k):
        send_reach(k).wait_send()


def local(G, D, reach, stake, hand_rank, hand_live, board_seqs, board_turn, seq_parent, set_parent):
    n = G * D
    own_seqs, boards, hands = reach.shape
    seqs = stake.shape[0]
    sets = set_parent.shape[0]
    tiles = -(-hands // LANE)
    width = tiles * LANE
    wide = -(-width // 256) * 256
    staged = jnp.transpose(reach.reshape(own_seqs, n, 2, hands), (1, 2, 0, 3)).reshape(n, 2 * own_seqs, hands)
    staged = jnp.pad(staged, ((0, 0), (0, 0), (0, width - hands)))
    index = children(seq_parent, sets, KIDS)
    kids = ((index // 4) * 8 + index % 4).reshape(-1)
    live = jnp.arange(seqs, dtype=jnp.int32)[None, :] < board_seqs[:, None]
    scale = jnp.where(live, stake[None, :], 0.0).reshape(2, n, own_seqs)
    scale = jnp.transpose(scale, (1, 0, 2)).reshape(n * 8, 1)
    turn_sets = sets // 4
    vmem = pl.BlockSpec(memory_space=pltpu.VMEM)
    smem = pl.BlockSpec(memory_space=pltpu.SMEM)
    river, best = pl.pallas_call(
        functools.partial(kernel, G, D, hands),
        out_shape=(
            jax.ShapeDtypeStruct((sets, 2, hands), jnp.float32),
            jax.ShapeDtypeStruct((turn_sets, TURNS, hands), jnp.float32),
        ),
        in_specs=[smem, smem, vmem, vmem, vmem, vmem, vmem, vmem],
        out_specs=(vmem, vmem),
        scratch_shapes=[
            pltpu.VMEM((n, 8, width), jnp.bfloat16),
            pltpu.VMEM((8, wide), jnp.float32),
            pltpu.VMEM((8, wide), jnp.int32),
            pltpu.VMEM((width, 8), jnp.float32),
            pltpu.VMEM((width, 8), jnp.int32),
            pltpu.VMEM((2, width, wide), jnp.bfloat16),
            pltpu.VMEM((n * 8, wide), jnp.float32),
            pltpu.VMEM((2, sets, width), jnp.float32),
            pltpu.VMEM((2 * n, sets, LANE), jnp.float32),
            pltpu.VMEM((TURNS, sets, LANE), jnp.float32),
            pltpu.VMEM((turn_sets, TURNS, width), jnp.float32),
            pltpu.SemaphoreType.DMA((n,)),
            pltpu.SemaphoreType.DMA((n,)),
            pltpu.SemaphoreType.DMA((tiles,)),
            pltpu.SemaphoreType.DMA((n,)),
            pltpu.SemaphoreType.DMA((tiles, D // 2 + G)),
            pltpu.SemaphoreType.DMA((tiles,)),
            pltpu.SemaphoreType.DMA((2,)),
        ],
        compiler_params=pltpu.CompilerParams(
            collective_id=0, has_side_effects=True, vmem_limit_bytes=56 << 20),
    )(kids, board_turn[:, 0], set_parent[:, None], staged, hand_rank, hand_live,
      jnp.asarray(card_bits(hands, wide)), scale)
    return river, best


def solution(mesh):
    axes = ("grp", "dev")
    in_specs = (
        P(axes, None, None),
        P(),
        P(axes, None),
        P(axes, None),
        P(axes),
        P(),
        P(),
        P(),
    )
    out_specs = (P(None, axes, None), P())
    body = functools.partial(local, mesh.shape["grp"], mesh.shape["dev"])
    return jax.shard_map(body, mesh=mesh, in_specs=in_specs, out_specs=out_specs, check_vma=False)
```

```python
import functools

import jax
import jax.numpy as jnp
import numpy as np
from jax import lax
from jax.experimental import pallas as pl
from jax.experimental.pallas import tpu as pltpu
from jax.sharding import PartitionSpec as P

TURNS = 16
KIDS = 8
LANE = 128
MESH = pl.DeviceIdType.MESH


def card_bits(count, padded):
    pairs = [(a, b) for a in range(52) for b in range(a + 1, 52)][:count]
    words = np.zeros((2, padded), np.int32)
    for hand, pair in enumerate(pairs):
        for card in pair:
            words[card // 26, hand] |= 1 << (card % 26)
    return words


def kernel(G, D, hands, turn_ref, board_seqs_ref, seq_parent_ref, set_parent_ref, stake_ref, reach_ref, rank_ref,
           live_ref, bits_ref,
           river_out, turn_out,
           kids_ref, scale_ref, parent_col, turn_rows, moved, dense, rows_f, rows_i, cols_f, cols_i, pay, leaf, river,
           packed, gathered, chance, best,
           send_a, recv_a, send_c, recv_c, send_e, recv_e, own_sem):
    n = G * D
    tiles = -(-hands // LANE)
    width = tiles * LANE
    sets = river_out.shape[0]
    turn_sets = turn_out.shape[0]
    g, d = lax.axis_index("grp"), lax.axis_index("dev")
    core = lax.rem(d, 2)
    me = g * D + d

    def where_is(flat):
        return (flat // D, lax.rem(flat, D))

    barrier = pltpu.get_barrier_semaphore()

    @pl.loop(1, n)
    def _(k):
        pl.semaphore_signal(barrier, inc=1, device_id=where_is(lax.rem(me + k, n)), device_id_type=MESH)

    pl.semaphore_wait(barrier, n - 1)

    bits = n.bit_length() - 1
    order = [2, 1] + [i for i in range(3, bits)] + [0]

    def partner(k):
        to = me
        for place, bit in enumerate(order):
            flip = lax.rem(k // (1 << place), 2)
            have = lax.rem(me // (1 << bit), 2)
            to = to + (flip - 2 * flip * have) * (1 << bit)
        return to

    def send_reach(k):
        to = partner(k)
        return pltpu.make_async_remote_copy(
            src_ref=reach_ref.at[to], dst_ref=moved.at[me], send_sem=send_a.at[k], recv_sem=recv_a.at[me],
            device_id=where_is(to), device_id_type=MESH)

    def got_reach(k):
        frm = lax.rem(me + k, n)
        return pltpu.make_async_remote_copy(
            src_ref=reach_ref.at[frm], dst_ref=moved.at[frm], send_sem=send_a.at[k], recv_sem=recv_a.at[frm],
            device_id=where_is(frm), device_id_type=MESH)

    own = pltpu.make_async_copy(reach_ref.at[me], moved.at[me], own_sem.at[0])
    own.start()

    @pl.loop(1, n)
    def _(k):
        send_reach(k).start()

    rows_f[...] = jnp.zeros_like(rows_f)
    rows_i[...] = jnp.zeros_like(rows_i)
    rows_f[0:2, 0:hands] = rank_ref[...].astype(jnp.float32)
    rows_i[0:2, 0:hands] = live_ref[...]
    dead = 1 - rows_i[0:2, :]
    low, high = bits_ref[0:1, :], bits_ref[1:2, :]
    ours = low + (1 << 26) + dead * (1 << 27)
    theirs = low + (1 << 27) + dead * (1 << 26)
    rows_i[0:2, :] = ours
    rows_i[2:3, :] = high
    rows_i[3:5, :] = theirs
    for tile in range(tiles):
        cut = slice(tile * LANE, (tile + 1) * LANE)
        cols_f[cut, :] = jnp.transpose(rows_f[:, cut])
        cols_i[cut, :] = jnp.transpose(rows_i[:, cut])

    @pl.loop(0, width // 16)
    def _(step):
        at = pl.ds(pl.multiple_of(step * 16, 16), 16)
        ranks, words = cols_f[at, :], cols_i[at, :]
        for board in range(2):
            shared = (rows_i[board:board + 1, :] & words[:, 3 + board:4 + board]) | (rows_i[2:3, :] & words[:, 2:3])
            sign = jnp.clip(rows_f[board:board + 1, :] - ranks[:, board:board + 1], -1.0, 1.0)
            pay[board, at, :] = jnp.where(shared == 0, sign, 0.0).astype(jnp.bfloat16)

    seq_parent = seq_parent_ref[...]

    @pl.loop(0, sets)
    def _(p):
        start = jnp.sum((seq_parent < p).astype(jnp.int32))
        last = jnp.sum((seq_parent <= p).astype(jnp.int32)) - 1
        for kid in range(KIDS):
            index = jnp.minimum(start + kid, last)
            kids_ref[p * KIDS + kid] = (index // 4) * 8 + lax.rem(index, 4)

    seqs = seq_parent.shape[1]

    @pl.loop(0, n)
    def _(src):
        row = lax.broadcasted_iota(jnp.int32, (8, 1), 0)
        seq = src * 4 + row % 4
        lane = lax.broadcasted_iota(jnp.int32, (8, seqs), 1)
        stake = jnp.sum(jnp.where(lane == seq, stake_ref[...], 0.0), axis=1, keepdims=True)
        limit = jnp.where(row < 4, board_seqs_ref[0], board_seqs_ref[1])
        scale_ref[pl.ds(pl.multiple_of(src * 8, 8), 8), :] = jnp.where(seq < limit, stake, 0.0)

    half = LANE // 2
    low_half = lax.broadcasted_iota(jnp.int32, (1, LANE), 1) < half

    @pl.loop(0, n)
    def _(src):
        turn_rows[pl.ds(src, 1), :] = jnp.where(low_half, turn_ref[2 * src], turn_ref[2 * src + 1])

    dense[...] = jnp.zeros_like(dense)
    set_row = lax.broadcasted_iota(jnp.int32, (sets, sets), 0)
    set_lane = lax.broadcasted_iota(jnp.int32, (sets, sets), 1)
    parent_col[...] = jnp.sum(jnp.where(set_row == set_lane, set_parent_ref[...], 0), axis=1, keepdims=True)

    own.wait()

    @pl.loop(1, n)
    def _(k):
        got_reach(k).wait_recv()

    chunk = 32
    first = lax.broadcasted_iota(jnp.int32, (chunk * 8, 1), 0) % 8 < 4

    @pl.loop(0, n // chunk)
    def _(part):
        src = pl.ds(part * chunk, chunk)
        dense[:, 0:hands] = moved[src].astype(jnp.float32).reshape(chunk * 8, hands).astype(jnp.bfloat16)
        rows = dense[...]
        at = pl.ds(pl.multiple_of(part * chunk * 8, chunk * 8), chunk * 8)
        scale = scale_ref[at, :]
        for nt in range(leaf.shape[1] // 256):
            cut = slice(nt * 256, (nt + 1) * 256)
            one = jnp.dot(rows, pay[0, :, cut], preferred_element_type=jnp.float32)
            two = jnp.dot(rows, pay[1, :, cut], preferred_element_type=jnp.float32)
            leaf[at, cut] = jnp.where(first, one, two) * scale

    @pl.loop(0, sets)
    def _(p):
        for board in range(2):
            row = leaf[pl.ds(kids_ref[p * KIDS] + 4 * board, 1), 0:width]
            for kid in range(1, KIDS):
                row = jnp.maximum(row, leaf[pl.ds(kids_ref[p * KIDS + kid] + 4 * board, 1), 0:width])
            river[board, pl.ds(p, 1), :] = row
            river_out[p, board:board + 1, :] = row[:, 0:hands]

    pieces = -(-hands // half)
    lines = D // 2
    for tile in range(tiles):
        one, two = (river[board, :, tile * LANE:(tile + 1) * LANE] for board in range(2))
        packed[2 * tile] = jnp.where(low_half, one, pltpu.roll(two, half, 1))
        packed[2 * tile + 1] = jnp.where(low_half, pltpu.roll(one, half, 1), two)

    def piece_of(grp, dev):
        return lax.rem(dev + D - 1, D) * G + grp

    mine = piece_of(g, d)

    def owner(piece):
        return (lax.rem(piece, G), lax.rem(piece // G + 1, D))

    def send_river(piece):
        return pltpu.make_async_remote_copy(
            src_ref=packed.at[piece], dst_ref=gathered.at[me], send_sem=send_c.at[piece], recv_sem=recv_c.at[me],
            device_id=owner(piece), device_id_type=MESH)

    @pl.loop(0, pieces)
    def _(piece):
        @pl.when(piece != mine)
        def _():
            send_river(piece).start()

    def send_turn(piece, slot, to):
        return pltpu.make_async_remote_copy(
            src_ref=best.at[piece], dst_ref=best.at[piece], send_sem=send_e.at[piece, slot], recv_sem=recv_e.at[piece],
            device_id=to, device_id_type=MESH)

    @pl.when(mine < pieces)
    def _():
        keep = pltpu.make_async_copy(packed.at[mine], gathered.at[me], own_sem.at[1])
        keep.start()
        keep.wait()

        @pl.loop(1, n)
        def _(k):
            frm = partner(k)
            pltpu.make_async_remote_copy(
                src_ref=packed.at[0], dst_ref=gathered.at[frm], send_sem=send_c.at[0], recv_sem=recv_c.at[frm],
                device_id=where_is(frm), device_id_type=MESH).wait_recv()

        group = 8
        psub = 32
        for turn0 in range(0, TURNS, group):
            for p0 in range(0, sets, psub):
                def add(src, accs):
                    block = gathered[src, p0:p0 + psub, :]
                    turn = jnp.broadcast_to(turn_rows[pl.ds(src, 1), :], (psub, LANE))
                    return tuple(acc + jnp.where(turn == turn0 + i, block, 0.0) for i, acc in enumerate(accs))
                accs = lax.fori_loop(
                    0, n, add, tuple(jnp.zeros((psub, LANE), jnp.float32) for _ in range(group)), unroll=4)
                for i in range(group):
                    chance[turn0 + i, p0:p0 + psub, :] = accs[i] + pltpu.roll(accs[i], half, 1)

        parents = jnp.broadcast_to(parent_col[...], (sets, LANE))

        @pl.loop(0, turn_sets)
        def _(q):
            chosen = parents == q
            rows = [jnp.max(jnp.where(chosen, chance[t], -jnp.inf), axis=0, keepdims=True) for t in range(TURNS)]
            early, late = jnp.concatenate(rows[:8], axis=0), jnp.concatenate(rows[8:], axis=0)
            best[mine, q] = jnp.where(low_half, early, late)

    line, core_of = d // 2, core

    def line_dev(k):
        return 2 * lax.rem(line + k, lines) + core_of

    def across(piece, run):
        for k in range(1, G):
            run(send_turn(piece, lines - 1 + k, (lax.rem(g + k, G), d)))

    def pair(piece, run):
        run(send_turn(piece, lines - 1 + G, (g, d + 1 - 2 * core)))

    def start(copy):
        copy.start()

    def finish(copy):
        copy.wait_send()

    def got(piece):
        send_turn(piece, 0, (lax.rem(g + 1, G), d)).wait_recv()

    @pl.when(mine < pieces)
    def _():
        for k in range(1, lines):
            start(send_turn(mine, k, (g, line_dev(k))))
        across(mine, start)
        pair(mine, start)

    @pl.loop(1, lines)
    def _(k):
        piece = piece_of(g, line_dev(k))

        @pl.when(piece < pieces)
        def _():
            got(piece)
            across(piece, start)
            pair(piece, start)

    @pl.loop(0, lines)
    def _(k):
        for j in range(1, G):
            piece = piece_of(lax.rem(g + j, G), line_dev(k))

            @pl.when(piece < pieces)
            def _():
                got(piece)
                pair(piece, start)

    @pl.loop(0, lines)
    def _(k):
        for j in range(G):
            piece = piece_of(lax.rem(g + j, G), line_dev(k) + 1 - 2 * core)

            @pl.when(piece < pieces)
            def _():
                got(piece)

    for tile in range(tiles):
        span = min(LANE, hands - tile * LANE)
        cut = slice(tile * LANE, tile * LANE + span)
        left = best[2 * tile]
        flipped = pltpu.roll(left, half, 2)
        if 2 * tile + 1 < pieces:
            right = best[2 * tile + 1]
            turn_out[:, 0:8, cut] = jnp.where(low_half, left, pltpu.roll(right, half, 2))[:, :, 0:span]
            turn_out[:, 8:16, cut] = jnp.where(low_half, flipped, right)[:, :, 0:span]
        else:
            turn_out[:, 0:8, cut] = left[:, :, 0:span]
            turn_out[:, 8:16, cut] = flipped[:, :, 0:span]

    @pl.when(mine < pieces)
    def _():
        for k in range(1, lines):
            finish(send_turn(mine, k, (g, line_dev(k))))

    @pl.loop(0, lines)
    def _(k):
        piece = piece_of(g, line_dev(k))

        @pl.when(piece < pieces)
        def _():
            across(piece, finish)

        for j in range(G):
            far = piece_of(lax.rem(g + j, G), line_dev(k))

            @pl.when(far < pieces)
            def _():
                pair(far, finish)

    @pl.loop(0, pieces)
    def _(piece):
        @pl.when(piece != mine)
        def _():
            send_river(piece).wait_send()

    @pl.loop(1, n)
    def _(k):
        send_reach(k).wait_send()


def local(G, D, reach, stake, hand_rank, hand_live, board_seqs, board_turn, seq_parent, set_parent):
    n = G * D
    own_seqs, boards, hands = reach.shape
    seqs = stake.shape[0]
    sets = set_parent.shape[0]
    tiles = -(-hands // LANE)
    width = tiles * LANE
    wide = -(-width // 256) * 256
    staged = jnp.transpose(reach.reshape(own_seqs, n, 2, hands), (1, 2, 0, 3)).reshape(n, 2 * own_seqs, hands)
    turn_sets = sets // 4
    vmem = pl.BlockSpec(memory_space=pltpu.VMEM)
    smem = pl.BlockSpec(memory_space=pltpu.SMEM)
    river, best = pl.pallas_call(
        functools.partial(kernel, G, D, hands),
        out_shape=(
            jax.ShapeDtypeStruct((sets, 2, hands), jnp.float32),
            jax.ShapeDtypeStruct((turn_sets, TURNS, hands), jnp.float32),
        ),
        in_specs=[smem, smem, vmem, vmem, vmem, vmem, vmem, vmem, vmem],
        out_specs=(vmem, vmem),
        scratch_shapes=[
            pltpu.SMEM((sets * KIDS,), jnp.int32),
            pltpu.VMEM((n * 8, 1), jnp.float32),
            pltpu.VMEM((sets, 1), jnp.int32),
            pltpu.VMEM((n, LANE), jnp.int32),
            pltpu.VMEM((n, 8, hands), jnp.bfloat16),
            pltpu.VMEM((256, width), jnp.bfloat16),
            pltpu.VMEM((8, wide), jnp.float32),
            pltpu.VMEM((8, wide), jnp.int32),
            pltpu.VMEM((width, 8), jnp.float32),
            pltpu.VMEM((width, 8), jnp.int32),
            pltpu.VMEM((2, width, wide), jnp.bfloat16),
            pltpu.VMEM((n * 8, wide), jnp.float32),
            pltpu.VMEM((2, sets, width), jnp.float32),
            pltpu.VMEM((2 * tiles, sets, LANE), jnp.float32),
            pltpu.VMEM((n, sets, LANE), jnp.float32),
            pltpu.VMEM((TURNS, sets, LANE), jnp.float32),
            pltpu.VMEM((2 * tiles, turn_sets, 8, LANE), jnp.float32),
            pltpu.SemaphoreType.DMA((n,)),
            pltpu.SemaphoreType.DMA((n,)),
            pltpu.SemaphoreType.DMA((2 * tiles,)),
            pltpu.SemaphoreType.DMA((n,)),
            pltpu.SemaphoreType.DMA((2 * tiles, D // 2 + G)),
            pltpu.SemaphoreType.DMA((2 * tiles,)),
            pltpu.SemaphoreType.DMA((2,)),
        ],
        compiler_params=pltpu.CompilerParams(
            collective_id=0, has_side_effects=True, vmem_limit_bytes=56 << 20),
    )(board_turn[:, 0], board_seqs, seq_parent[None, :], set_parent[None, :], stake[None, :], staged,
      hand_rank, hand_live, jnp.asarray(card_bits(hands, wide)))
    return river, best


def solution(mesh):
    axes = ("grp", "dev")
    in_specs = (
        P(axes, None, None),
        P(),
        P(axes, None),
        P(axes, None),
        P(axes),
        P(),
        P(),
        P(),
    )
    out_specs = (P(None, axes, None), P())
    body = functools.partial(local, mesh.shape["grp"], mesh.shape["dev"])
    return jax.shard_map(body, mesh=mesh, in_specs=in_specs, out_specs=out_specs, check_vma=False)
```

```python
import functools

import jax
import jax.numpy as jnp
import numpy as np
from jax import lax
from jax.experimental import pallas as pl
from jax.experimental.pallas import tpu as pltpu
from jax.sharding import PartitionSpec as P

TURNS = 16
KIDS = 8
LANE = 128
MESH = pl.DeviceIdType.MESH


def card_bits(count, padded):
    pairs = [(a, b) for a in range(52) for b in range(a + 1, 52)][:count]
    words = np.zeros((2, padded), np.int32)
    for hand, pair in enumerate(pairs):
        for card in pair:
            words[card // 26, hand] |= 1 << (card % 26)
    return words


def kernel(G, D, hands, turn_ref, board_seqs_ref, seq_parent_ref, set_parent_ref, stake_ref, reach_ref, rank_ref,
           live_ref, bits_ref,
           river_out, turn_out,
           kids_ref, scale_ref, parent_col, turn_rows, moved, dense, rows_f, rows_i, cols_f, cols_i, pay, leaf, river,
           packed, gathered, chance, best,
           send_a, recv_a, send_c, recv_c, send_e, recv_e, own_sem):
    n = G * D
    tiles = -(-hands // LANE)
    width = tiles * LANE
    sets = river_out.shape[0]
    turn_sets = turn_out.shape[0]
    g, d = lax.axis_index("grp"), lax.axis_index("dev")
    core = lax.rem(d, 2)
    me = g * D + d

    def where_is(flat):
        return (flat // D, lax.rem(flat, D))

    barrier = pltpu.get_barrier_semaphore()

    @pl.loop(1, n)
    def _(k):
        pl.semaphore_signal(barrier, inc=1, device_id=where_is(lax.rem(me + k, n)), device_id_type=MESH)

    pl.semaphore_wait(barrier, n - 1)

    bits = n.bit_length() - 1
    order = [2, 1] + [i for i in range(3, bits)] + [0]

    def partner(k):
        to = me
        for place, bit in enumerate(order):
            flip = lax.rem(k // (1 << place), 2)
            have = lax.rem(me // (1 << bit), 2)
            to = to + (flip - 2 * flip * have) * (1 << bit)
        return to

    def send_reach(k):
        to = partner(k)
        return pltpu.make_async_remote_copy(
            src_ref=reach_ref.at[to], dst_ref=moved.at[me], send_sem=send_a.at[k], recv_sem=recv_a.at[me],
            device_id=where_is(to), device_id_type=MESH)

    def got_reach(k):
        frm = lax.rem(me + k, n)
        return pltpu.make_async_remote_copy(
            src_ref=reach_ref.at[frm], dst_ref=moved.at[frm], send_sem=send_a.at[k], recv_sem=recv_a.at[frm],
            device_id=where_is(frm), device_id_type=MESH)

    own = pltpu.make_async_copy(reach_ref.at[me], moved.at[me], own_sem.at[0])
    own.start()

    @pl.loop(1, n)
    def _(k):
        send_reach(k).start()

    rows_f[...] = jnp.zeros_like(rows_f)
    rows_i[...] = jnp.zeros_like(rows_i)
    rows_f[0:2, 0:hands] = rank_ref[...].astype(jnp.float32)
    rows_i[0:2, 0:hands] = live_ref[...]
    dead = 1 - rows_i[0:2, :]
    low, high = bits_ref[0:1, :], bits_ref[1:2, :]
    ours = low + (1 << 26) + dead * (1 << 27)
    theirs = low + (1 << 27) + dead * (1 << 26)
    rows_i[0:2, :] = ours
    rows_i[2:3, :] = high
    rows_i[3:5, :] = theirs
    for tile in range(tiles):
        cut = slice(tile * LANE, (tile + 1) * LANE)
        cols_f[cut, :] = jnp.transpose(rows_f[:, cut])
        cols_i[cut, :] = jnp.transpose(rows_i[:, cut])

    @pl.loop(0, width // 16)
    def _(step):
        at = pl.ds(pl.multiple_of(step * 16, 16), 16)
        ranks, words = cols_f[at, :], cols_i[at, :]
        for board in range(2):
            shared = (rows_i[board:board + 1, :] & words[:, 3 + board:4 + board]) | (rows_i[2:3, :] & words[:, 2:3])
            sign = jnp.clip(rows_f[board:board + 1, :] - ranks[:, board:board + 1], -1.0, 1.0)
            pay[board, at, :] = jnp.where(shared == 0, sign, 0.0).astype(jnp.bfloat16)

    seq_parent = seq_parent_ref[...]

    block = 16

    @pl.loop(0, sets // block)
    def _(step):
        p0 = step * block
        starts = [jnp.sum((seq_parent < p0 + i).astype(jnp.int32)) for i in range(block + 1)]
        for i in range(block):
            for kid in range(KIDS):
                index = jnp.minimum(starts[i] + kid, starts[i + 1] - 1)
                kids_ref[(p0 + i) * KIDS + kid] = index + (index // 4) * 4

    seqs = seq_parent.shape[1]
    row = lax.broadcasted_iota(jnp.int32, (n * 8, 1), 0)
    seq = (row >> 3) * 4 + (row & 3)
    lane = lax.broadcasted_iota(jnp.int32, (n * 8, seqs), 1)
    stake = jnp.sum(jnp.where(lane == seq, stake_ref[...], 0.0), axis=1, keepdims=True)
    limit = jnp.where((row & 4) == 0, board_seqs_ref[0], board_seqs_ref[1])
    scale_ref[...] = jnp.where(seq < limit, stake, 0.0)

    half = LANE // 2
    low_half = lax.broadcasted_iota(jnp.int32, (1, LANE), 1) < half

    @pl.loop(0, n)
    def _(src):
        turn_rows[pl.ds(src, 1), :] = jnp.where(low_half, turn_ref[2 * src], turn_ref[2 * src + 1])

    dense[...] = jnp.zeros_like(dense)
    set_row = lax.broadcasted_iota(jnp.int32, (sets, sets), 0)
    set_lane = lax.broadcasted_iota(jnp.int32, (sets, sets), 1)
    parent_col[...] = jnp.sum(jnp.where(set_row == set_lane, set_parent_ref[...], 0), axis=1, keepdims=True)

    own.wait()

    @pl.loop(1, n)
    def _(k):
        got_reach(k).wait_recv()

    chunk = 32
    first = lax.broadcasted_iota(jnp.int32, (chunk * 8, 1), 0) % 8 < 4

    @pl.loop(0, n // chunk)
    def _(part):
        src = pl.ds(part * chunk, chunk)
        dense[:, 0:hands] = moved[src].astype(jnp.float32).reshape(chunk * 8, hands).astype(jnp.bfloat16)
        rows = dense[...]
        at = pl.ds(pl.multiple_of(part * chunk * 8, chunk * 8), chunk * 8)
        scale = scale_ref[at, :]
        for nt in range(leaf.shape[1] // 256):
            cut = slice(nt * 256, (nt + 1) * 256)
            one = jnp.dot(rows, pay[0, :, cut], preferred_element_type=jnp.float32)
            two = jnp.dot(rows, pay[1, :, cut], preferred_element_type=jnp.float32)
            leaf[at, cut] = jnp.where(first, one, two) * scale

    @pl.loop(0, sets)
    def _(p):
        for board in range(2):
            row = leaf[pl.ds(kids_ref[p * KIDS] + 4 * board, 1), 0:width]
            for kid in range(1, KIDS):
                row = jnp.maximum(row, leaf[pl.ds(kids_ref[p * KIDS + kid] + 4 * board, 1), 0:width])
            river[board, pl.ds(p, 1), :] = row
            river_out[p, board:board + 1, :] = row[:, 0:hands]

    pieces = -(-hands // half)
    lines = D // 2
    for tile in range(tiles):
        one, two = (river[board, :, tile * LANE:(tile + 1) * LANE] for board in range(2))
        packed[2 * tile] = jnp.where(low_half, one, pltpu.roll(two, half, 1))
        packed[2 * tile + 1] = jnp.where(low_half, pltpu.roll(one, half, 1), two)

    def piece_of(grp, dev):
        return lax.rem(dev + D - 1, D) * G + grp

    mine = piece_of(g, d)

    def owner(piece):
        return (lax.rem(piece, G), lax.rem(piece // G + 1, D))

    def send_river(piece):
        return pltpu.make_async_remote_copy(
            src_ref=packed.at[piece], dst_ref=gathered.at[me], send_sem=send_c.at[piece], recv_sem=recv_c.at[me],
            device_id=owner(piece), device_id_type=MESH)

    @pl.loop(0, pieces)
    def _(piece):
        @pl.when(piece != mine)
        def _():
            send_river(piece).start()

    def send_turn(piece, slot, to):
        return pltpu.make_async_remote_copy(
            src_ref=best.at[piece], dst_ref=best.at[piece], send_sem=send_e.at[piece, slot], recv_sem=recv_e.at[piece],
            device_id=to, device_id_type=MESH)

    @pl.when(mine < pieces)
    def _():
        keep = pltpu.make_async_copy(packed.at[mine], gathered.at[me], own_sem.at[1])
        keep.start()
        keep.wait()

        @pl.loop(1, n)
        def _(k):
            frm = partner(k)
            pltpu.make_async_remote_copy(
                src_ref=packed.at[0], dst_ref=gathered.at[frm], send_sem=send_c.at[0], recv_sem=recv_c.at[frm],
                device_id=where_is(frm), device_id_type=MESH).wait_recv()

        group = 8
        psub = 32
        for turn0 in range(0, TURNS, group):
            for p0 in range(0, sets, psub):
                def add(src, accs):
                    block = gathered[src, p0:p0 + psub, :]
                    turn = jnp.broadcast_to(turn_rows[pl.ds(src, 1), :], (psub, LANE))
                    return tuple(acc + jnp.where(turn == turn0 + i, block, 0.0) for i, acc in enumerate(accs))
                accs = lax.fori_loop(
                    0, n, add, tuple(jnp.zeros((psub, LANE), jnp.float32) for _ in range(group)), unroll=4)
                for i in range(group):
                    chance[turn0 + i, p0:p0 + psub, :] = accs[i] + pltpu.roll(accs[i], half, 1)

        parents = jnp.broadcast_to(parent_col[...], (sets, LANE))

        @pl.loop(0, turn_sets)
        def _(q):
            chosen = parents == q
            rows = [jnp.max(jnp.where(chosen, chance[t], -jnp.inf), axis=0, keepdims=True) for t in range(TURNS)]
            early, late = jnp.concatenate(rows[:8], axis=0), jnp.concatenate(rows[8:], axis=0)
            best[mine, q] = jnp.where(low_half, early, late)

    line, core_of = d // 2, core

    def line_dev(k):
        return 2 * lax.rem(line + k, lines) + core_of

    def across(piece, run):
        for k in range(1, G):
            run(send_turn(piece, lines - 1 + k, (lax.rem(g + k, G), d)))

    def pair(piece, run):
        run(send_turn(piece, lines - 1 + G, (g, d + 1 - 2 * core)))

    def start(copy):
        copy.start()

    def finish(copy):
        copy.wait_send()

    def got(piece):
        send_turn(piece, 0, (lax.rem(g + 1, G), d)).wait_recv()

    @pl.when(mine < pieces)
    def _():
        for k in range(1, lines):
            start(send_turn(mine, k, (g, line_dev(k))))
        across(mine, start)
        pair(mine, start)

    @pl.loop(1, lines)
    def _(k):
        piece = piece_of(g, line_dev(k))

        @pl.when(piece < pieces)
        def _():
            got(piece)
            across(piece, start)
            pair(piece, start)

    @pl.loop(0, lines)
    def _(k):
        for j in range(1, G):
            piece = piece_of(lax.rem(g + j, G), line_dev(k))

            @pl.when(piece < pieces)
            def _():
                got(piece)
                pair(piece, start)

    @pl.loop(0, lines)
    def _(k):
        for j in range(G):
            piece = piece_of(lax.rem(g + j, G), line_dev(k) + 1 - 2 * core)

            @pl.when(piece < pieces)
            def _():
                got(piece)

    for tile in range(tiles):
        span = min(LANE, hands - tile * LANE)
        cut = slice(tile * LANE, tile * LANE + span)
        left = best[2 * tile]
        flipped = pltpu.roll(left, half, 2)
        if 2 * tile + 1 < pieces:
            right = best[2 * tile + 1]
            turn_out[:, 0:8, cut] = jnp.where(low_half, left, pltpu.roll(right, half, 2))[:, :, 0:span]
            turn_out[:, 8:16, cut] = jnp.where(low_half, flipped, right)[:, :, 0:span]
        else:
            turn_out[:, 0:8, cut] = left[:, :, 0:span]
            turn_out[:, 8:16, cut] = flipped[:, :, 0:span]

    @pl.when(mine < pieces)
    def _():
        for k in range(1, lines):
            finish(send_turn(mine, k, (g, line_dev(k))))

    @pl.loop(0, lines)
    def _(k):
        piece = piece_of(g, line_dev(k))

        @pl.when(piece < pieces)
        def _():
            across(piece, finish)

        for j in range(G):
            far = piece_of(lax.rem(g + j, G), line_dev(k))

            @pl.when(far < pieces)
            def _():
                pair(far, finish)

    @pl.loop(0, pieces)
    def _(piece):
        @pl.when(piece != mine)
        def _():
            send_river(piece).wait_send()

    @pl.loop(1, n)
    def _(k):
        send_reach(k).wait_send()


def local(G, D, reach, stake, hand_rank, hand_live, board_seqs, board_turn, seq_parent, set_parent):
    n = G * D
    own_seqs, boards, hands = reach.shape
    seqs = stake.shape[0]
    sets = set_parent.shape[0]
    tiles = -(-hands // LANE)
    width = tiles * LANE
    wide = -(-width // 256) * 256
    staged = jnp.transpose(reach.reshape(own_seqs, n, 2, hands), (1, 2, 0, 3)).reshape(n, 2 * own_seqs, hands)
    turn_sets = sets // 4
    vmem = pl.BlockSpec(memory_space=pltpu.VMEM)
    smem = pl.BlockSpec(memory_space=pltpu.SMEM)
    river, best = pl.pallas_call(
        functools.partial(kernel, G, D, hands),
        out_shape=(
            jax.ShapeDtypeStruct((sets, 2, hands), jnp.float32),
            jax.ShapeDtypeStruct((turn_sets, TURNS, hands), jnp.float32),
        ),
        in_specs=[smem, smem, vmem, vmem, vmem, vmem, vmem, vmem, vmem],
        out_specs=(vmem, vmem),
        scratch_shapes=[
            pltpu.SMEM((sets * KIDS,), jnp.int32),
            pltpu.VMEM((n * 8, 1), jnp.float32),
            pltpu.VMEM((sets, 1), jnp.int32),
            pltpu.VMEM((n, LANE), jnp.int32),
            pltpu.VMEM((n, 8, hands), jnp.bfloat16),
            pltpu.VMEM((256, width), jnp.bfloat16),
            pltpu.VMEM((8, wide), jnp.float32),
            pltpu.VMEM((8, wide), jnp.int32),
            pltpu.VMEM((width, 8), jnp.float32),
            pltpu.VMEM((width, 8), jnp.int32),
            pltpu.VMEM((2, width, wide), jnp.bfloat16),
            pltpu.VMEM((n * 8, wide), jnp.float32),
            pltpu.VMEM((2, sets, width), jnp.float32),
            pltpu.VMEM((2 * tiles, sets, LANE), jnp.float32),
            pltpu.VMEM((n, sets, LANE), jnp.float32),
            pltpu.VMEM((TURNS, sets, LANE), jnp.float32),
            pltpu.VMEM((2 * tiles, turn_sets, 8, LANE), jnp.float32),
            pltpu.SemaphoreType.DMA((n,)),
            pltpu.SemaphoreType.DMA((n,)),
            pltpu.SemaphoreType.DMA((2 * tiles,)),
            pltpu.SemaphoreType.DMA((n,)),
            pltpu.SemaphoreType.DMA((2 * tiles, D // 2 + G)),
            pltpu.SemaphoreType.DMA((2 * tiles,)),
            pltpu.SemaphoreType.DMA((2,)),
        ],
        compiler_params=pltpu.CompilerParams(
            collective_id=0, has_side_effects=True, vmem_limit_bytes=56 << 20),
    )(board_turn[:, 0], board_seqs, seq_parent[None, :], set_parent[None, :], stake[None, :], staged,
      hand_rank, hand_live, jnp.asarray(card_bits(hands, wide)))
    return river, best


def solution(mesh):
    axes = ("grp", "dev")
    in_specs = (
        P(axes, None, None),
        P(),
        P(axes, None),
        P(axes, None),
        P(axes),
        P(),
        P(),
        P(),
    )
    out_specs = (P(None, axes, None), P())
    body = functools.partial(local, mesh.shape["grp"], mesh.shape["dev"])
    return jax.shard_map(body, mesh=mesh, in_specs=in_specs, out_specs=out_specs, check_vma=False)
```

```python
import functools

import jax
import jax.numpy as jnp
import numpy as np
from jax import lax
from jax.experimental import pallas as pl
from jax.experimental.pallas import tpu as pltpu
from jax.sharding import PartitionSpec as P

TURNS = 16
KIDS = 8
LANE = 128
MESH = pl.DeviceIdType.MESH


def card_bits(count, padded):
    pairs = [(a, b) for a in range(52) for b in range(a + 1, 52)][:count]
    words = np.zeros((2, padded), np.int32)
    for hand, pair in enumerate(pairs):
        for card in pair:
            words[card // 26, hand] |= 1 << (card % 26)
    return words


def kernel(G, D, hands, turn_ref, board_seqs_ref, seq_parent_ref, set_parent_ref, stake_ref, reach_ref, rank_ref,
           live_ref, bits_ref,
           river_out, turn_out,
           kids_ref, scale_ref, parent_col, turn_rows, moved, dense, rows_f, rows_i, cols_f, cols_i, pay, leaf, river,
           packed, gathered, chance, best,
           send_a, recv_a, send_c, recv_c, send_e, recv_e, own_sem):
    n = G * D
    tiles = -(-hands // LANE)
    width = tiles * LANE
    sets = river_out.shape[0]
    turn_sets = turn_out.shape[0]
    g, d = lax.axis_index("grp"), lax.axis_index("dev")
    core = lax.rem(d, 2)
    me = g * D + d

    def where_is(flat):
        return (flat // D, lax.rem(flat, D))

    barrier = pltpu.get_barrier_semaphore()

    @pl.loop(1, n)
    def _(k):
        pl.semaphore_signal(barrier, inc=1, device_id=where_is(lax.rem(me + k, n)), device_id_type=MESH)

    pl.semaphore_wait(barrier, n - 1)

    bits = n.bit_length() - 1
    order = [2, 1] + [i for i in range(3, bits)] + [0]

    def partner(k):
        to = me
        for place, bit in enumerate(order):
            flip = lax.rem(k // (1 << place), 2)
            have = lax.rem(me // (1 << bit), 2)
            to = to + (flip - 2 * flip * have) * (1 << bit)
        return to

    def send_reach(k):
        to = partner(k)
        return pltpu.make_async_remote_copy(
            src_ref=reach_ref.at[to], dst_ref=moved.at[me], send_sem=send_a.at[k], recv_sem=recv_a.at[me],
            device_id=where_is(to), device_id_type=MESH)

    def got_reach(k):
        frm = lax.rem(me + k, n)
        return pltpu.make_async_remote_copy(
            src_ref=reach_ref.at[frm], dst_ref=moved.at[frm], send_sem=send_a.at[k], recv_sem=recv_a.at[frm],
            device_id=where_is(frm), device_id_type=MESH)

    own = pltpu.make_async_copy(reach_ref.at[me], moved.at[me], own_sem.at[0])
    own.start()

    @pl.loop(1, n)
    def _(k):
        send_reach(k).start()

    rows_f[...] = jnp.zeros_like(rows_f)
    rows_i[...] = jnp.zeros_like(rows_i)
    rows_f[0:2, 0:hands] = rank_ref[...].astype(jnp.float32)
    rows_i[0:2, 0:hands] = live_ref[...]
    dead = 1 - rows_i[0:2, :]
    low, high = bits_ref[0:1, :], bits_ref[1:2, :]
    ours = low + (1 << 26) + dead * (1 << 27)
    theirs = low + (1 << 27) + dead * (1 << 26)
    rows_i[0:2, :] = ours
    rows_i[2:3, :] = high
    rows_i[3:5, :] = theirs
    for tile in range(tiles):
        cut = slice(tile * LANE, (tile + 1) * LANE)
        cols_f[cut, :] = jnp.transpose(rows_f[:, cut])
        cols_i[cut, :] = jnp.transpose(rows_i[:, cut])

    @pl.loop(0, width // 16)
    def _(step):
        at = pl.ds(pl.multiple_of(step * 16, 16), 16)
        ranks, words = cols_f[at, :], cols_i[at, :]
        for board in range(2):
            shared = (rows_i[board:board + 1, :] & words[:, 3 + board:4 + board]) | (rows_i[2:3, :] & words[:, 2:3])
            sign = jnp.clip(rows_f[board:board + 1, :] - ranks[:, board:board + 1], -1.0, 1.0)
            pay[board, at, :] = jnp.where(shared == 0, sign, 0.0).astype(jnp.bfloat16)

    seq_parent = seq_parent_ref[...]

    block = 16

    @pl.loop(0, sets // block)
    def _(step):
        p0 = step * block
        starts = [jnp.sum((seq_parent < p0 + i).astype(jnp.int32)) for i in range(block + 1)]
        for i in range(block):
            for kid in range(KIDS):
                index = jnp.minimum(starts[i] + kid, starts[i + 1] - 1)
                kids_ref[(p0 + i) * KIDS + kid] = index + (index // 4) * 4

    seqs = seq_parent.shape[1]
    row = lax.broadcasted_iota(jnp.int32, (n * 8, 1), 0)
    seq = (row >> 3) * 4 + (row & 3)
    lane = lax.broadcasted_iota(jnp.int32, (n * 8, seqs), 1)
    stake = jnp.sum(jnp.where(lane == seq, stake_ref[...], 0.0), axis=1, keepdims=True)
    limit = jnp.where((row & 4) == 0, board_seqs_ref[0], board_seqs_ref[1])
    scale_ref[...] = jnp.where(seq < limit, stake, 0.0)

    half = LANE // 2
    low_half = lax.broadcasted_iota(jnp.int32, (1, LANE), 1) < half

    @pl.loop(0, n)
    def _(src):
        turn_rows[pl.ds(src, 1), :] = jnp.where(low_half, turn_ref[2 * src], turn_ref[2 * src + 1])

    dense[...] = jnp.zeros_like(dense)
    set_row = lax.broadcasted_iota(jnp.int32, (sets, sets), 0)
    set_lane = lax.broadcasted_iota(jnp.int32, (sets, sets), 1)
    parent_col[...] = jnp.sum(jnp.where(set_row == set_lane, set_parent_ref[...], 0), axis=1, keepdims=True)

    own.wait()

    @pl.loop(1, n)
    def _(k):
        got_reach(k).wait_recv()

    chunk = 32
    first = lax.broadcasted_iota(jnp.int32, (chunk * 8, 1), 0) % 8 < 4

    @pl.loop(0, n // chunk)
    def _(part):
        src = pl.ds(part * chunk, chunk)
        dense[:, 0:hands] = moved[src].astype(jnp.float32).reshape(chunk * 8, hands).astype(jnp.bfloat16)
        rows = dense[...]
        at = pl.ds(pl.multiple_of(part * chunk * 8, chunk * 8), chunk * 8)
        scale = scale_ref[at, :]
        for nt in range(leaf.shape[1] // 256):
            cut = slice(nt * 256, (nt + 1) * 256)
            one = jnp.dot(rows, pay[0, :, cut], preferred_element_type=jnp.float32)
            two = jnp.dot(rows, pay[1, :, cut], preferred_element_type=jnp.float32)
            leaf[at, cut] = jnp.where(first, one, two) * scale

    @pl.loop(0, sets)
    def _(p):
        for board in range(2):
            row = leaf[pl.ds(kids_ref[p * KIDS] + 4 * board, 1), 0:width]
            for kid in range(1, KIDS):
                row = jnp.maximum(row, leaf[pl.ds(kids_ref[p * KIDS + kid] + 4 * board, 1), 0:width])
            river[board, pl.ds(p, 1), :] = row
            river_out[p, board:board + 1, :] = row[:, 0:hands]

    pieces = -(-hands // half)
    lines = D // 2
    for tile in range(tiles):
        one, two = (river[board, :, tile * LANE:(tile + 1) * LANE] for board in range(2))
        packed[2 * tile] = jnp.where(low_half, one, pltpu.roll(two, half, 1))
        packed[2 * tile + 1] = jnp.where(low_half, pltpu.roll(one, half, 1), two)

    def piece_of(grp, dev):
        return lax.rem(dev + D - 1, D) * G + grp

    mine = piece_of(g, d)

    def owner(piece):
        return (lax.rem(piece, G), lax.rem(piece // G + 1, D))

    def send_river(piece):
        return pltpu.make_async_remote_copy(
            src_ref=packed.at[piece], dst_ref=gathered.at[me], send_sem=send_c.at[piece], recv_sem=recv_c.at[me],
            device_id=owner(piece), device_id_type=MESH)

    @pl.loop(0, pieces)
    def _(piece):
        @pl.when(piece != mine)
        def _():
            send_river(piece).start()

    def send_turn(piece, slot, to):
        return pltpu.make_async_remote_copy(
            src_ref=best.at[piece], dst_ref=best.at[piece], send_sem=send_e.at[piece, slot], recv_sem=recv_e.at[piece],
            device_id=to, device_id_type=MESH)

    @pl.when(mine < pieces)
    def _():
        keep = pltpu.make_async_copy(packed.at[mine], gathered.at[me], own_sem.at[1])
        keep.start()
        keep.wait()

        @pl.loop(1, n)
        def _(k):
            frm = partner(k)
            pltpu.make_async_remote_copy(
                src_ref=packed.at[0], dst_ref=gathered.at[frm], send_sem=send_c.at[0], recv_sem=recv_c.at[frm],
                device_id=where_is(frm), device_id_type=MESH).wait_recv()

        group = 8
        psub = 32
        for turn0 in range(0, TURNS, group):
            for p0 in range(0, sets, psub):
                def add(src, accs):
                    block = gathered[src, p0:p0 + psub, :]
                    turn = jnp.broadcast_to(turn_rows[pl.ds(src, 1), :], (psub, LANE))
                    return tuple(acc + jnp.where(turn == turn0 + i, block, 0.0) for i, acc in enumerate(accs))
                accs = lax.fori_loop(
                    0, n, add, tuple(jnp.zeros((psub, LANE), jnp.float32) for _ in range(group)), unroll=4)
                for i in range(group):
                    chance[turn0 + i, p0:p0 + psub, :] = accs[i] + pltpu.roll(accs[i], half, 1)

        parents = jnp.broadcast_to(parent_col[...], (sets, LANE))

        @pl.loop(0, turn_sets)
        def _(q):
            chosen = parents == q
            rows = [jnp.max(jnp.where(chosen, chance[t], -jnp.inf), axis=0, keepdims=True) for t in range(TURNS)]
            early, late = jnp.concatenate(rows[:8], axis=0), jnp.concatenate(rows[8:], axis=0)
            best[mine, q] = jnp.where(low_half, early, late)

    line, core_of = d // 2, core

    def line_dev(k):
        return 2 * lax.rem(line + k, lines) + core_of

    def across(piece, run):
        for k in range(1, G):
            run(send_turn(piece, lines - 1 + k, (lax.rem(g + k, G), d)))

    def pair(piece, run):
        run(send_turn(piece, lines - 1 + G, (g, d + 1 - 2 * core)))

    def start(copy):
        copy.start()

    def finish(copy):
        copy.wait_send()

    def got(piece):
        send_turn(piece, 0, (lax.rem(g + 1, G), d)).wait_recv()

    @pl.when(mine < pieces)
    def _():
        for k in range(1, lines):
            start(send_turn(mine, k, (g, line_dev(k))))
        across(mine, start)
        pair(mine, start)

    @pl.loop(1, lines)
    def _(k):
        piece = piece_of(g, line_dev(k))

        @pl.when(piece < pieces)
        def _():
            got(piece)
            pair(piece, start)
            across(piece, start)

    @pl.loop(0, lines)
    def _(k):
        for j in range(1, G):
            piece = piece_of(lax.rem(g + j, G), line_dev(k))

            @pl.when(piece < pieces)
            def _():
                got(piece)
                pair(piece, start)

    @pl.loop(0, lines)
    def _(k):
        for j in range(G):
            piece = piece_of(lax.rem(g + j, G), line_dev(k) + 1 - 2 * core)

            @pl.when(piece < pieces)
            def _():
                got(piece)

    for tile in range(tiles):
        span = min(LANE, hands - tile * LANE)
        cut = slice(tile * LANE, tile * LANE + span)
        left = best[2 * tile]
        flipped = pltpu.roll(left, half, 2)
        if 2 * tile + 1 < pieces:
            right = best[2 * tile + 1]
            turn_out[:, 0:8, cut] = jnp.where(low_half, left, pltpu.roll(right, half, 2))[:, :, 0:span]
            turn_out[:, 8:16, cut] = jnp.where(low_half, flipped, right)[:, :, 0:span]
        else:
            turn_out[:, 0:8, cut] = left[:, :, 0:span]
            turn_out[:, 8:16, cut] = flipped[:, :, 0:span]

    @pl.when(mine < pieces)
    def _():
        for k in range(1, lines):
            finish(send_turn(mine, k, (g, line_dev(k))))

    @pl.loop(0, lines)
    def _(k):
        piece = piece_of(g, line_dev(k))

        @pl.when(piece < pieces)
        def _():
            across(piece, finish)

        for j in range(G):
            far = piece_of(lax.rem(g + j, G), line_dev(k))

            @pl.when(far < pieces)
            def _():
                pair(far, finish)

    @pl.loop(0, pieces)
    def _(piece):
        @pl.when(piece != mine)
        def _():
            send_river(piece).wait_send()

    @pl.loop(1, n)
    def _(k):
        send_reach(k).wait_send()


def local(G, D, reach, stake, hand_rank, hand_live, board_seqs, board_turn, seq_parent, set_parent):
    n = G * D
    own_seqs, boards, hands = reach.shape
    seqs = stake.shape[0]
    sets = set_parent.shape[0]
    tiles = -(-hands // LANE)
    width = tiles * LANE
    wide = -(-width // 256) * 256
    staged = jnp.transpose(reach.reshape(own_seqs, n, 2, hands), (1, 2, 0, 3)).reshape(n, 2 * own_seqs, hands)
    turn_sets = sets // 4
    vmem = pl.BlockSpec(memory_space=pltpu.VMEM)
    smem = pl.BlockSpec(memory_space=pltpu.SMEM)
    river, best = pl.pallas_call(
        functools.partial(kernel, G, D, hands),
        out_shape=(
            jax.ShapeDtypeStruct((sets, 2, hands), jnp.float32),
            jax.ShapeDtypeStruct((turn_sets, TURNS, hands), jnp.float32),
        ),
        in_specs=[smem, smem, vmem, vmem, vmem, pl.BlockSpec(memory_space=pl.ANY), vmem, vmem, vmem],
        out_specs=(vmem, vmem),
        scratch_shapes=[
            pltpu.SMEM((sets * KIDS,), jnp.int32),
            pltpu.VMEM((n * 8, 1), jnp.float32),
            pltpu.VMEM((sets, 1), jnp.int32),
            pltpu.VMEM((n, LANE), jnp.int32),
            pltpu.VMEM((n, 8, hands), jnp.bfloat16),
            pltpu.VMEM((256, width), jnp.bfloat16),
            pltpu.VMEM((8, wide), jnp.float32),
            pltpu.VMEM((8, wide), jnp.int32),
            pltpu.VMEM((width, 8), jnp.float32),
            pltpu.VMEM((width, 8), jnp.int32),
            pltpu.VMEM((2, width, wide), jnp.bfloat16),
            pltpu.VMEM((n * 8, wide), jnp.float32),
            pltpu.VMEM((2, sets, width), jnp.float32),
            pltpu.VMEM((2 * tiles, sets, LANE), jnp.float32),
            pltpu.VMEM((n, sets, LANE), jnp.float32),
            pltpu.VMEM((TURNS, sets, LANE), jnp.float32),
            pltpu.VMEM((2 * tiles, turn_sets, 8, LANE), jnp.float32),
            pltpu.SemaphoreType.DMA((n,)),
            pltpu.SemaphoreType.DMA((n,)),
            pltpu.SemaphoreType.DMA((2 * tiles,)),
            pltpu.SemaphoreType.DMA((n,)),
            pltpu.SemaphoreType.DMA((2 * tiles, D // 2 + G)),
            pltpu.SemaphoreType.DMA((2 * tiles,)),
            pltpu.SemaphoreType.DMA((2,)),
        ],
        compiler_params=pltpu.CompilerParams(
            collective_id=0, has_side_effects=True, vmem_limit_bytes=56 << 20),
    )(board_turn[:, 0], board_seqs, seq_parent[None, :], set_parent[None, :], stake[None, :], staged,
      hand_rank, hand_live, jnp.asarray(card_bits(hands, wide)))
    return river, best


def solution(mesh):
    axes = ("grp", "dev")
    in_specs = (
        P(axes, None, None),
        P(),
        P(axes, None),
        P(axes, None),
        P(axes),
        P(),
        P(),
        P(),
    )
    out_specs = (P(None, axes, None), P())
    body = functools.partial(local, mesh.shape["grp"], mesh.shape["dev"])
    return jax.shard_map(body, mesh=mesh, in_specs=in_specs, out_specs=out_specs, check_vma=False)
```
